32 devices in a mesh: grp: 2 (over y), atoms: 4 (over z), feat: 2 (over x), rep: 2 (over core).
Axes of the slice: x: 2, y: 2, z: 4, core: 2. Of those that a mesh axis runs over, the one named last changes fastest.
Arguments:
- atom_coords: bfloat16 [4, 2048, 3, 3072], P(('grp', 'rep'), None, None, 'atoms'), parts along dimension 0, may hold values from -9 to 9
- atom_pairs: int32 [2, 1024], P(None, 'feat'), may hold values from 0 to 3071, as said below
- traj_ids: int32 [4, 2048], P(('grp', 'rep')), parts along dimension 0, may hold values from 0 to 7, never falling along the last dimension, each value on 1 to 512 neighbouring positions
Outputs:
- corr_inst: float32 [2048, 1024], P(('grp', 'atoms', 'rep'), 'feat'), parts along dimension 0
- corr_lag: float32 [2048, 1024], P(('grp', 'atoms', 'rep'), 'feat'), parts along dimension 0
- projections: float32 [4, 2048, 1024], P(('grp', 'rep'), 'atoms', 'feat'), parts along dimension 0
The draws below stay inside these ranges and needn't reach their ends.
There are 2 independent parts, one for each index of `grp`. The reference program is written for one: setup_inputs(seed, part) draws one part's arguments, and reference() takes and returns one part's arrays. A program takes and returns all parts, laid end to end along the dimension named above; an argument that names none is the same for every part. Nothing has to cross between parts.
Inputs may be any that keep to these rules, and one draw needn't show every extreme that they name: `atom_pairs`: the two atoms of a feature differ. `traj_ids`: trajectory numbers never fall along a replica stream; some trajectory holds exactly 512 frames.
All inputs are finite; a program needn't handle non-finite values.
Results may differ from the reference program's by a relative error of at most 0.0003.
Values may be sent and summed in bfloat16 or wider, within the bound.
A program may use at most 128 MiB of HBM per device.

```python
import math
import jax
import jax.numpy as jnp
import numpy as np
from jax import lax

ATOMS = 3072
FEATS = 1024
LAG = 10
TRAJS = 8
REPLICAS = 2
FRAMES = 2048


def draw_atom_coords(key, part):
    keys = jax.random.split(key, 10)
    base = jax.random.uniform(keys[0], (1, 1, 3, ATOMS), jnp.float32, -5.0, 5.0)
    times = jnp.arange(FRAMES, dtype=jnp.float32).reshape(1, FRAMES, 1, 1)
    envelope = 0.5 + times / FRAMES
    periods = jnp.exp(jax.random.uniform(keys[1], (3,), jnp.float32, math.log(40.0), math.log(400.0)))
    amplitudes = jax.random.uniform(keys[2], (3, 1, 1, 3, ATOMS), jnp.float32, 0.05, 0.35)
    phases = jax.random.uniform(keys[3], (3, REPLICAS, 1, 3, ATOMS), jnp.float32, -math.pi, math.pi)
    motion = jnp.zeros((REPLICAS, FRAMES, 3, ATOMS), jnp.float32)
    for mode in range(3):
        motion = motion + amplitudes[mode] * jnp.sin(2.0 * math.pi * times / periods[mode] + phases[mode])
    own_periods = jnp.exp(jax.random.uniform(keys[7], (1, 1, 3, ATOMS), jnp.float32, math.log(40.0), math.log(400.0)))
    own_amps = jnp.exp(jax.random.uniform(keys[8], (1, 1, 3, ATOMS), jnp.float32, math.log(0.3), math.log(0.8)))
    own_phases = jax.random.uniform(keys[9], (REPLICAS, 1, 3, ATOMS), jnp.float32, -math.pi, math.pi)
    own_motion = own_amps * jnp.sin(2.0 * math.pi * times / own_periods + own_phases)
    spread = jnp.exp(jax.random.uniform(keys[4], (1, 1, 1, ATOMS), jnp.float32, math.log(0.05), math.log(0.3)))
    noise = jax.random.truncated_normal(keys[6], -3.0, 3.0, (REPLICAS, FRAMES, 3, ATOMS), jnp.float32) * spread
    return (base + envelope * motion + own_motion + noise).astype(jnp.bfloat16)


def draw_atom_pairs(key, part):
    keys = jax.random.split(key, 2)
    first = jax.random.randint(keys[0], (FEATS,), 0, ATOMS, jnp.int32)
    first = first.at[0].set(ATOMS - 1).at[1].set(0)
    offset = jax.random.randint(keys[1], (FEATS,), 1, ATOMS, jnp.int32)
    second = (first + offset) % ATOMS
    return jnp.stack([first, second]).astype(jnp.int32)


def split_up(amount, total, most, skew):
    weights = [(1 << 20) // math.isqrt(rank ** skew) + 1 for rank in range(2, amount + 1)]
    surplus, counts = total - most - (amount - 1), [1] * (amount - 1)
    while surplus > 0:
        movable = [i for i in range(amount - 1) if counts[i] < most]
        whole, budget = sum([weights[i] for i in movable]), surplus
        for i in movable:
            extra = min(most - counts[i], max(1, budget * weights[i] // whole), surplus)
            counts[i] = counts[i] + extra
            surplus = surplus - extra
    return np.array([most] + counts)


def ragged(own_key, amount, total, most, skew):
    if amount == 2:
        one = jax.random.randint(own_key, (), max(1, total - most), min(most, total - 1) + 1)
        return jnp.stack([one, total - one])
    tallies = jnp.asarray(split_up(amount, total, most, skew), jnp.int32)
    twos = (amount - 1) // 2
    source_of, taker = tallies[1:1 + 2 * twos:2], tallies[2:2 + 2 * twos:2]
    margin = jnp.minimum(source_of - 1, most - taker)
    shifted = jax.random.randint(jax.random.fold_in(own_key, 1), (twos,), 0, 1 << 20) % (margin + 1)
    tallies = tallies.at[1:1 + 2 * twos:2].set(source_of - shifted).at[2:2 + 2 * twos:2].set(taker + shifted)
    return tallies[jax.random.permutation(jax.random.fold_in(own_key, 2), amount)]


def setup_inputs(seed: int = 0, part: int = 0) -> dict:
    arg_keys = jax.random.split(jax.random.key(seed), 4)
    own_keys = jax.random.split(jax.random.fold_in(arg_keys[3], part), 4)
    return {
        "atom_coords": draw_atom_coords(jax.random.fold_in(jax.random.fold_in(arg_keys[3], part), 71), part),
        "atom_pairs": draw_atom_pairs(jax.random.fold_in(arg_keys[3], 71), part),
        "traj_ids": jax.vmap(lambda own: jnp.searchsorted(jnp.cumsum(ragged(own, TRAJS, FRAMES, FRAMES // 4, 1)), jnp.arange(FRAMES), side="right"))(jax.random.split(own_keys[2], REPLICAS)).reshape((REPLICAS, FRAMES)).astype(jnp.int32),
    }


def featurize(positions, pairs):
    first = jnp.take(positions, pairs[0], axis=2)
    second = jnp.take(positions, pairs[1], axis=2)
    delta = first - second
    return jnp.sqrt(lax.optimization_barrier(jnp.sum(delta * delta, axis=1)) + 0.01)

def cross_moment(left, right):
    return lax.dot_general(left, right, (((0,), (0,)), ((), ())), precision=lax.Precision.HIGHEST, preferred_element_type=jnp.float32)

def reference(atom_coords, atom_pairs, traj_ids):
    padding = jnp.full((LAG,), -1, jnp.int32)
    present_list = []
    future_list = []
    valid_list = []
    for replica in range(REPLICAS):
        positions = atom_coords[replica].astype(jnp.float32)
        current = featurize(positions, atom_pairs)
        future = jnp.concatenate([current[LAG:], jnp.zeros((LAG, FEATS), jnp.float32)], 0)
        ids = jnp.concatenate([traj_ids[replica].astype(jnp.int32), padding])
        valid = (ids[:FRAMES] == ids[LAG:]).astype(jnp.float32)[:, None]
        present_list.append(current)
        future_list.append(future)
        valid_list.append(valid)
    count = jnp.float32(0.0)
    total_now = jnp.zeros((FEATS,), jnp.float32)
    total_next = jnp.zeros((FEATS,), jnp.float32)
    for replica in range(REPLICAS):
        count = count + jnp.sum(valid_list[replica])
        total_now = total_now + lax.optimization_barrier(jnp.sum(valid_list[replica] * present_list[replica], 0))
        total_next = total_next + lax.optimization_barrier(jnp.sum(valid_list[replica] * future_list[replica], 0))
    mean_now = total_now / count
    mean_next = total_next / count
    moment_inst = jnp.zeros((FEATS, FEATS), jnp.float32)
    moment_lag = jnp.zeros((FEATS, FEATS), jnp.float32)
    spread_now = jnp.zeros((FEATS,), jnp.float32)
    spread_next = jnp.zeros((FEATS,), jnp.float32)
    centered_list = []
    for replica in range(REPLICAS):
        centered = present_list[replica] - mean_now
        future_centered = future_list[replica] - mean_next
        valid = valid_list[replica]
        moment_inst = moment_inst + cross_moment(centered, valid * centered)
        moment_lag = moment_lag + cross_moment(centered, valid * future_centered)
        spread_now = spread_now + lax.optimization_barrier(jnp.sum(valid * centered * centered, 0))
        spread_next = spread_next + lax.optimization_barrier(jnp.sum(valid * future_centered * future_centered, 0))
        centered_list.append(centered)
    scale_now = 1.0 / jnp.sqrt(spread_now / count + 1e-05)
    scale_next = 1.0 / jnp.sqrt(spread_next / count + 1e-05)
    corr_inst = moment_inst / count * scale_now[:, None] * scale_now[None, :]
    corr_lag = moment_lag / count * scale_now[:, None] * scale_next[None, :]
    projections = jnp.stack([centered * scale_now for centered in centered_list])
    return (corr_inst, corr_lag, projections)
```

```python
import math

import jax
import jax.numpy as jnp
from jax import lax
from jax.sharding import PartitionSpec as P

LAG = 10


def matmul(left, right, dims, precision=None):
    return lax.dot_general(
        left, right, (dims, ((), ())), precision=precision, preferred_element_type=jnp.float32
    )


def slots_per_pass(width, refs, atoms):
    share = width * (1.0 - math.exp(-refs / atoms)) + 2.05 * math.sqrt(width)
    return min(-(-width // 16) * 16, -(-int(share) // 16) * 16)


def shards(atom_coords, atom_pairs, traj_ids):
    groups = lax.axis_size("atoms")
    feat_groups = lax.axis_size("feat")
    frames = atom_coords.shape[1]
    frames_here = frames // groups
    part = frames_here // feat_groups
    width = atom_coords.shape[3]
    cols = atom_pairs.shape[1]
    z = lax.axis_index("atoms")
    x = lax.axis_index("feat")

    pairs = lax.all_gather(atom_pairs, "feat", axis=1, tiled=True)
    feats = pairs.shape[1]
    refs = pairs.reshape(-1)
    room = slots_per_pass(width, 2 * feats, width * groups)

    atom_no = jnp.arange(groups * width, dtype=jnp.int32).reshape(groups, width)
    hit = atom_no[:, :, None] == refs[None, None, :]
    used = jnp.any(hit, axis=2)
    before = (jnp.arange(width)[:, None] < jnp.arange(width)[None, :]).astype(jnp.bfloat16)
    rank = matmul(used.astype(jnp.bfloat16), before, ((1,), (0,)))
    most = jnp.max(jnp.sum(used.astype(jnp.float32), 1))
    ref_rank = jnp.sum(jnp.where(hit, rank[:, :, None], 0.0), axis=(0, 1)).reshape(2, feats)
    ref_shard = pairs // width
    used_own = lax.dynamic_index_in_dim(used, z, 0, False)
    rank_own = lax.dynamic_index_in_dim(rank, z, 0, False)

    grouped = jnp.transpose(atom_coords[0], (1, 0, 2)).reshape(3, groups, feat_groups, part, width)
    blocks = lax.dynamic_index_in_dim(grouped, x, 2, False)

    def deltas(turn):
        first = turn * jnp.float32(room)
        slot = jnp.arange(room, dtype=jnp.float32) + first
        pick = ((rank_own[None, :] == slot[:, None]) & used_own[None, :]).astype(jnp.bfloat16)
        chosen = lax.dot_general(
            pick, blocks, (((1,), (3,)), ((), ())), preferred_element_type=jnp.float32
        ).astype(jnp.bfloat16)
        chosen = jnp.transpose(chosen, (2, 1, 0, 3))
        got = lax.all_to_all(chosen, "atoms", split_axis=0, concat_axis=0, tiled=True)
        shard_no = jnp.arange(groups, dtype=jnp.int32)
        place = (ref_rank[:, None, :, None] == slot) & (ref_shard[:, None, :, None] == shard_no[:, None, None])
        sign = place[0].astype(jnp.bfloat16) - place[1].astype(jnp.bfloat16)
        total = 0.0
        for s in range(groups):
            total = total + lax.dot_general(
                sign[s], got[s], (((1,), (1,)), ((), ())), preferred_element_type=jnp.float32
            )
        return total

    delta = deltas(jnp.float32(0.0))
    _, delta = lax.while_loop(
        lambda c: c[0] * room < most, lambda c: (c[0] + 1.0, c[1] + deltas(c[0])), (jnp.float32(1.0), delta)
    )
    computed = jnp.sqrt(jnp.sum(delta * delta, axis=1) + 0.01).T

    every = lax.all_gather(computed, "feat", axis=0, tiled=True)
    own = lax.dynamic_slice_in_dim(every, x * cols, cols, 1)
    route = [(i, i - 1) for i in range(1, groups)]
    incoming = lax.ppermute(own[:LAG], "atoms", route)
    future = jnp.concatenate([own[LAG:], incoming], 0)

    ids = jnp.concatenate([traj_ids[0], jnp.full((LAG,), -1, jnp.int32)])
    ids_now = lax.dynamic_slice_in_dim(ids, z * frames_here, frames_here)
    ids_later = lax.dynamic_slice_in_dim(ids, z * frames_here + LAG, frames_here)
    valid = (ids_now == ids_later).astype(jnp.float32)[:, None]

    count_b = jnp.sum(valid)
    inverse = 1.0 / jnp.maximum(count_b, 1.0)
    now_b = jnp.sum(valid * every, 0) * inverse
    next_b = jnp.sum(valid * future, 0) * inverse
    now_c = valid * (every - now_b)
    next_c = valid * (future - next_b)
    own_c = lax.dynamic_slice_in_dim(now_c, x * cols, cols, 1)
    stats = jnp.concatenate(
        [now_b, next_b, jnp.sum(now_c * now_c, 0), jnp.sum(next_c * next_c, 0), jnp.full((128,), count_b)]
    )
    stats = lax.all_gather(stats, ("atoms", "rep"), axis=0, tiled=False)

    local = matmul(now_c, jnp.concatenate([own_c, next_c], 1), ((0,), (0,)), lax.Precision.HIGH)
    mine = lax.psum_scatter(local, ("atoms", "rep"), scatter_dimension=0, tiled=True)

    counts = stats[:, -1:]
    now_all = stats[:, :feats]
    next_all = stats[:, feats : feats + cols]
    sq_now = stats[:, feats + cols : 2 * feats + cols]
    sq_next = stats[:, 2 * feats + cols : 2 * feats + 2 * cols]
    count = jnp.sum(counts)
    mean_now = jnp.sum(counts * now_all, 0) / count
    mean_next = jnp.sum(counts * next_all, 0) / count
    off_now = now_all - mean_now
    off_next = next_all - mean_next
    spread_now = jnp.sum(sq_now + counts * off_now * off_now, 0)
    spread_next = jnp.sum(sq_next + counts * off_next * off_next, 0)
    scale_now = 1.0 / jnp.sqrt(spread_now / count + 1e-05)
    scale_next = 1.0 / jnp.sqrt(spread_next / count + 1e-05)

    rows = feats // lax.axis_size(("atoms", "rep"))
    row = lax.axis_index(("atoms", "rep")) * rows
    off_rows = lax.dynamic_slice_in_dim(off_now, row, rows, 1)
    off_cols = lax.dynamic_slice_in_dim(off_now, x * cols, cols, 1)
    mine = mine + matmul(
        counts * off_rows, jnp.concatenate([off_cols, off_next], 1), ((0,), (0,)), lax.Precision.HIGHEST
    )
    scale_rows = lax.dynamic_slice_in_dim(scale_now, row, rows)
    scale_cols = lax.dynamic_slice_in_dim(scale_now, x * cols, cols)
    mean_cols = lax.dynamic_slice_in_dim(mean_now, x * cols, cols)
    corr_inst = mine[:, :cols] / count * scale_rows[:, None] * scale_cols[None, :]
    corr_lag = mine[:, cols:] / count * scale_rows[:, None] * scale_next[None, :]
    projections = ((own - mean_cols) * scale_cols)[None]
    return (corr_inst, corr_lag, projections)


def solution(mesh):
    placed = (P(("grp", "rep"), None, None, "atoms"), P(None, "feat"), P(("grp", "rep"), None))
    return jax.shard_map(
        shards,
        mesh=mesh,
        in_specs=placed,
        out_specs=(
            P(("grp", "atoms", "rep"), "feat"),
            P(("grp", "atoms", "rep"), "feat"),
            P(("grp", "rep"), "atoms", "feat"),
        ),
        check_vma=False,
    )
```

```python
import functools
import math

import jax
import jax.numpy as jnp
from jax import lax
from jax.experimental import pallas as pl
from jax.experimental.pallas import tpu as pltpu
from jax.sharding import PartitionSpec as P

LAG = 10


def matmul(left, right, dims, precision=None):
    return lax.dot_general(
        left, right, (dims, ((), ())), precision=precision, preferred_element_type=jnp.float32
    )

MESH = pl.DeviceIdType.MESH


def exchange_kernel(groups, feat_groups, room, lanes, chunks, tile, chosen, slots, out, sign, recv, *sems):
    z_send, z_recv, z_own, x_send, x_recv = sems
    z, x = lax.axis_index("atoms"), lax.axis_index("feat")
    half = groups // 2
    z_steps = [half] + [o for o in range(groups - 1, 0, -1) if o != half] if groups > 1 else []
    x_steps = list(range(1, feat_groups))
    tiles = out.shape[0] // tile
    barrier = pltpu.get_barrier_semaphore()
    for o in z_steps:
        pl.semaphore_signal(barrier, 1, device_id={"atoms": lax.rem(z + o, groups)}, device_id_type=MESH)
    for o in x_steps:
        pl.semaphore_signal(barrier, 1, device_id={"feat": lax.rem(x + o, feat_groups)}, device_id_type=MESH)
    pl.semaphore_wait(barrier, len(z_steps) + len(x_steps))

    here = pl.ds(pl.multiple_of(z * room, 16), room)
    z_copies = []
    for ch in range(chunks):
        row = []
        for i, o in enumerate(z_steps):
            dest = lax.rem(z + o, groups)
            row.append(
                pltpu.make_async_remote_copy(
                    src_ref=chosen.at[dest, ch],
                    dst_ref=recv.at[ch, here],
                    send_sem=z_send.at[ch, i],
                    recv_sem=z_recv.at[ch, i],
                    device_id={"atoms": dest},
                    device_id_type=MESH,
                )
            )
            row[-1].start()
        z_copies.append(row)
    own_copies = [pltpu.make_async_copy(chosen.at[z, ch], recv.at[ch, here], z_own.at[ch]) for ch in range(chunks)]
    for copy in own_copies:
        copy.start()

    place = lax.broadcasted_iota(jnp.int32, (128, groups * room), 1)

    def make_sign(i, carry):
        rows = pl.ds(pl.multiple_of(i * 128, 128), 128)
        pair = slots[rows, :]
        value = jnp.where(place == pair[:, 0:1], 1.0, 0.0) - jnp.where(place == pair[:, 1:2], 1.0, 0.0)
        sign[rows, :] = value.astype(jnp.bfloat16)
        return carry

    lax.fori_loop(0, out.shape[0] // 128, make_sign, 0)

    def x_copy(ch, i, k, o):
        part = out.at[
            pl.ds(pl.multiple_of(i * tile, tile), tile),
            pl.ds(pl.multiple_of((x * chunks + ch) * lanes, lanes), lanes),
        ]
        return pltpu.make_async_remote_copy(
            src_ref=part,
            dst_ref=part,
            send_sem=x_send.at[ch, i, k],
            recv_sem=x_recv.at[ch, i, k],
            device_id={"feat": lax.rem(x + o, feat_groups)},
            device_id_type=MESH,
        )

    for ch in range(chunks):
        own_copies[ch].wait()
        for copy in z_copies[ch]:
            copy.wait_recv()

        def features(i, carry, ch=ch):
            rows = pl.ds(pl.multiple_of(i * tile, tile), tile)
            delta = jnp.dot(sign[rows, :], recv[ch], preferred_element_type=jnp.float32)
            square = delta * delta
            total = square[:, :lanes] + square[:, lanes : 2 * lanes] + square[:, 2 * lanes :]
            cols = pl.ds(pl.multiple_of((x * chunks + ch) * lanes, lanes), lanes)
            out[rows, cols] = jnp.sqrt(total + 0.01)
            for k, o in enumerate(x_steps):
                x_copy(ch, i, k, o).start()
            return carry

        lax.fori_loop(0, tiles, features, 0)

    for ch in range(chunks):
        for copy in z_copies[ch]:
            copy.wait_send()

        def finish(i, carry, ch=ch):
            for k, o in enumerate(x_steps):
                x_copy(ch, i, k, o).wait()
            return carry

        lax.fori_loop(0, tiles, finish, 0)


def exchange(chosen, slots, groups, feat_groups):
    chunks, room, lanes = chosen.shape[1], chosen.shape[2], chosen.shape[3] // 3
    feats = slots.shape[0]
    tile = min(256, feats)
    vmem = pl.BlockSpec(memory_space=pltpu.VMEM)
    z_count, x_count = max(groups - 1, 1), max(feat_groups - 1, 1)
    dma = pltpu.SemaphoreType.DMA
    return pl.pallas_call(
        functools.partial(exchange_kernel, groups, feat_groups, room, lanes, chunks, tile),
        out_shape=jax.ShapeDtypeStruct((feats, feat_groups * chunks * lanes), jnp.float32),
        in_specs=[vmem, vmem],
        out_specs=vmem,
        scratch_shapes=[
            pltpu.VMEM((feats, groups * room), jnp.bfloat16),
            pltpu.VMEM((chunks, groups * room, 3 * lanes), jnp.bfloat16),
            dma((chunks, z_count)),
            dma((chunks, z_count)),
            dma((chunks,)),
            dma((chunks, feats // tile, x_count)),
            dma((chunks, feats // tile, x_count)),
        ],
        compiler_params=pltpu.CompilerParams(
            collective_id=0, has_side_effects=True, vmem_limit_bytes=48 * 1024 * 1024
        ),
    )(chosen, slots)


def slots_per_pass(width, refs, atoms):
    share = width * (1.0 - math.exp(-refs / atoms)) + 2.05 * math.sqrt(width)
    return min(-(-width // 16) * 16, -(-int(share) // 16) * 16)


def shards(atom_coords, atom_pairs, traj_ids):
    groups = lax.axis_size("atoms")
    feat_groups = lax.axis_size("feat")
    frames = atom_coords.shape[1]
    frames_here = frames // groups
    part = frames_here // feat_groups
    width = atom_coords.shape[3]
    cols = atom_pairs.shape[1]
    z = lax.axis_index("atoms")
    x = lax.axis_index("feat")

    pairs = lax.all_gather(atom_pairs, "feat", axis=1, tiled=True)
    feats = pairs.shape[1]
    refs = pairs.reshape(-1)
    room = slots_per_pass(width, 2 * feats, width * groups)

    atom_no = jnp.arange(groups * width, dtype=jnp.int32).reshape(groups, width)
    hit = atom_no[:, :, None] == refs[None, None, :]
    used = jnp.any(hit, axis=2)
    before = (jnp.arange(width)[:, None] < jnp.arange(width)[None, :]).astype(jnp.bfloat16)
    rank = matmul(used.astype(jnp.bfloat16), before, ((1,), (0,)))
    most = jnp.max(jnp.sum(used.astype(jnp.float32), 1))
    ref_rank = jnp.sum(jnp.where(hit, rank[:, :, None], 0.0), axis=(0, 1)).reshape(2, feats)
    ref_shard = pairs // width
    used_own = lax.dynamic_index_in_dim(used, z, 0, False)
    rank_own = lax.dynamic_index_in_dim(rank, z, 0, False)

    grouped = jnp.transpose(atom_coords[0], (1, 0, 2)).reshape(3, groups, feat_groups, part, width)
    blocks = lax.dynamic_index_in_dim(grouped, x, 2, False)

    lanes = 128 if part % 128 == 0 else part
    chunks = part // lanes

    def select(turn):
        slot = jnp.arange(room, dtype=jnp.float32) + turn * jnp.float32(room)
        pick = ((rank_own[None, :] == slot[:, None]) & used_own[None, :]).astype(jnp.bfloat16)
        chosen = lax.dot_general(
            pick, blocks, (((1,), (3,)), ((), ())), preferred_element_type=jnp.float32
        ).astype(jnp.bfloat16)
        chosen = jnp.transpose(chosen.reshape(room, 3, groups, chunks, lanes), (2, 3, 0, 1, 4))
        spot = ref_rank - turn * jnp.float32(room)
        inside = (spot >= 0) & (spot < room)
        spot = jnp.where(inside, ref_shard * room + spot.astype(jnp.int32), -1)
        return chosen.reshape(groups, chunks, room, 3 * lanes), spot.T

    def one_pass():
        return exchange(*select(jnp.float32(0.0)), groups, feat_groups)

    def more_passes():
        def step(carry):
            turn, delta = carry
            chosen, spot = select(turn)
            got = lax.all_to_all(chosen, "atoms", split_axis=0, concat_axis=0, tiled=True)
            got = jnp.transpose(got, (0, 2, 1, 3)).reshape(groups * room, chunks * 3 * lanes)
            place = jnp.arange(groups * room, dtype=jnp.int32)
            sign = (spot[:, :1] == place).astype(jnp.bfloat16) - (spot[:, 1:] == place).astype(jnp.bfloat16)
            return turn + 1.0, delta + matmul(sign, got, ((1,), (0,)))

        _, delta = lax.while_loop(
            lambda c: c[0] * room < most,
            step,
            (jnp.float32(0.0), jnp.zeros((feats, chunks * 3 * lanes), jnp.float32)),
        )
        delta = delta.reshape(feats, chunks, 3, lanes)
        computed = jnp.sqrt(jnp.sum(delta * delta, axis=2) + 0.01).reshape(feats, part)
        return lax.all_gather(computed, "feat", axis=1, tiled=True)

    every = lax.cond(most <= room, one_pass, more_passes).T
    own = lax.dynamic_slice_in_dim(every, x * cols, cols, 1)
    route = [(i, i - 1) for i in range(1, groups)]
    incoming = lax.ppermute(own[:LAG], "atoms", route)
    future = jnp.concatenate([own[LAG:], incoming], 0)

    ids = jnp.concatenate([traj_ids[0], jnp.full((LAG,), -1, jnp.int32)])
    ids_now = lax.dynamic_slice_in_dim(ids, z * frames_here, frames_here)
    ids_later = lax.dynamic_slice_in_dim(ids, z * frames_here + LAG, frames_here)
    valid = (ids_now == ids_later).astype(jnp.float32)[:, None]

    count_b = jnp.sum(valid)
    inverse = 1.0 / jnp.maximum(count_b, 1.0)
    now_b = jnp.sum(valid * every, 0) * inverse
    next_b = jnp.sum(valid * future, 0) * inverse
    now_c = valid * (every - now_b)
    next_c = valid * (future - next_b)
    own_c = lax.dynamic_slice_in_dim(now_c, x * cols, cols, 1)
    stats = jnp.concatenate(
        [now_b, next_b, jnp.sum(now_c * now_c, 0), jnp.sum(next_c * next_c, 0), jnp.full((128,), count_b)]
    )
    stats = lax.all_gather(stats, ("atoms", "rep"), axis=0, tiled=False)

    local = matmul(now_c, jnp.concatenate([own_c, next_c], 1), ((0,), (0,)), lax.Precision.HIGH)
    mine = lax.psum_scatter(local, ("atoms", "rep"), scatter_dimension=0, tiled=True)

    counts = stats[:, -1:]
    now_all = stats[:, :feats]
    next_all = stats[:, feats : feats + cols]
    sq_now = stats[:, feats + cols : 2 * feats + cols]
    sq_next = stats[:, 2 * feats + cols : 2 * feats + 2 * cols]
    count = jnp.sum(counts)
    mean_now = jnp.sum(counts * now_all, 0) / count
    mean_next = jnp.sum(counts * next_all, 0) / count
    off_now = now_all - mean_now
    off_next = next_all - mean_next
    spread_now = jnp.sum(sq_now + counts * off_now * off_now, 0)
    spread_next = jnp.sum(sq_next + counts * off_next * off_next, 0)
    scale_now = 1.0 / jnp.sqrt(spread_now / count + 1e-05)
    scale_next = 1.0 / jnp.sqrt(spread_next / count + 1e-05)

    rows = feats // lax.axis_size(("atoms", "rep"))
    row = lax.axis_index(("atoms", "rep")) * rows
    off_rows = lax.dynamic_slice_in_dim(off_now, row, rows, 1)
    off_cols = lax.dynamic_slice_in_dim(off_now, x * cols, cols, 1)
    mine = mine + matmul(
        counts * off_rows, jnp.concatenate([off_cols, off_next], 1), ((0,), (0,)), lax.Precision.HIGHEST
    )
    scale_rows = lax.dynamic_slice_in_dim(scale_now, row, rows)
    scale_cols = lax.dynamic_slice_in_dim(scale_now, x * cols, cols)
    mean_cols = lax.dynamic_slice_in_dim(mean_now, x * cols, cols)
    corr_inst = mine[:, :cols] / count * scale_rows[:, None] * scale_cols[None, :]
    corr_lag = mine[:, cols:] / count * scale_rows[:, None] * scale_next[None, :]
    projections = ((own - mean_cols) * scale_cols)[None]
    return (corr_inst, corr_lag, projections)


def solution(mesh):
    placed = (P(("grp", "rep"), None, None, "atoms"), P(None, "feat"), P(("grp", "rep"), None))
    return jax.shard_map(
        shards,
        mesh=mesh,
        in_specs=placed,
        out_specs=(
            P(("grp", "atoms", "rep"), "feat"),
            P(("grp", "atoms", "rep"), "feat"),
            P(("grp", "rep"), "atoms", "feat"),
        ),
        check_vma=False,
    )
```

```python
import functools
import math

import jax
import jax.numpy as jnp
from jax import lax
from jax.experimental import pallas as pl
from jax.experimental.pallas import tpu as pltpu
from jax.sharding import PartitionSpec as P

LAG = 10
HALO = 16


def matmul(left, right, dims, precision=None):
    return lax.dot_general(
        left, right, (dims, ((), ())), precision=precision, preferred_element_type=jnp.float32
    )

MESH = pl.DeviceIdType.MESH


def exchange_kernel(
    groups, feat_groups, room, lanes, chunks, tile, coords, picked, slots, out, halo, *scratch
):
    blocks, pick, chosen, sign, recv, edge, load, z_send, z_recv, z_own, x_send, x_recv, h_send, h_recv = scratch
    z, x = lax.axis_index("atoms"), lax.axis_index("feat")
    half = groups // 2
    z_steps = [half] + [o for o in range(groups - 1, 0, -1) if o != half] if groups > 1 else []
    x_steps = list(range(1, feat_groups))
    tiles = out.shape[0] // tile
    frames_here = feat_groups * chunks * lanes
    cols = halo.shape[1]
    z_dests = [lax.rem(z + o, groups) for o in z_steps] + [z]
    loads = []
    for ch in range(chunks):
        row = []
        for i, dest in enumerate(z_dests):
            start = pl.multiple_of(dest * frames_here + (x * chunks + ch) * lanes, 16)
            row.append(
                pltpu.make_async_copy(coords.at[:, pl.ds(start, lanes), :], blocks.at[ch, i], load.at[ch, i])
            )
            row[-1].start()
        loads.append(row)
    barrier = pltpu.get_barrier_semaphore()
    for o in z_steps:
        pl.semaphore_signal(barrier, 1, device_id={"atoms": lax.rem(z + o, groups)}, device_id_type=MESH)
    for o in x_steps:
        pl.semaphore_signal(barrier, 1, device_id={"feat": lax.rem(x + o, feat_groups)}, device_id_type=MESH)
    z_up, z_down = lax.rem(z + 1, groups), lax.rem(z + groups - 1, groups)

    @pl.when(x == 0)
    def _():
        for k in x_steps:
            pl.semaphore_signal(barrier, 1, device_id={"atoms": z_down, "feat": k}, device_id_type=MESH)

    @pl.when(x != 0)
    def _():
        pl.semaphore_signal(barrier, 1, device_id={"atoms": z_up, "feat": 0}, device_id_type=MESH)

    width = picked.shape[1]
    slot_no = lax.broadcasted_iota(jnp.int32, (room, width), 0)
    pick[...] = jnp.where(slot_no == picked[...], 1.0, 0.0).astype(jnp.bfloat16)

    @pl.when(x == 0)
    def _():
        pl.semaphore_wait(barrier, len(z_steps) + 2 * len(x_steps))

    @pl.when(x != 0)
    def _():
        pl.semaphore_wait(barrier, len(z_steps) + len(x_steps) + 1)

    def fill(ch, i):
        loads[ch][i].wait()
        for c in range(3):
            got = lax.dot_general(
                pick[...], blocks[ch, i, c], (((1,), (1,)), ((), ())), preferred_element_type=jnp.float32
            )
            chosen[ch, i, :, c * lanes : (c + 1) * lanes] = got.astype(jnp.bfloat16)

    here = pl.ds(pl.multiple_of(z * room, 16), room)
    z_copies = []
    for ch in range(chunks):
        row = []
        for i, o in enumerate(z_steps):
            fill(ch, i)
            row.append(
                pltpu.make_async_remote_copy(
                    src_ref=chosen.at[ch, i],
                    dst_ref=recv.at[ch, here],
                    send_sem=z_send.at[ch, i],
                    recv_sem=z_recv.at[ch, i],
                    device_id={"atoms": z_dests[i]},
                    device_id_type=MESH,
                )
            )
            row[-1].start()
        z_copies.append(row)
    own_copies = []
    for ch in range(chunks):
        fill(ch, len(z_steps))
        own_copies.append(
            pltpu.make_async_copy(chosen.at[ch, len(z_steps)], recv.at[ch, here], z_own.at[ch])
        )
        own_copies[-1].start()

    place = lax.broadcasted_iota(jnp.int32, (128, groups * room), 1)

    def make_sign(i, carry):
        rows = pl.ds(pl.multiple_of(i * 128, 128), 128)
        pair = slots[rows, :]
        value = jnp.where(place == pair[:, 0:1], 1.0, 0.0) - jnp.where(place == pair[:, 1:2], 1.0, 0.0)
        sign[rows, :] = value.astype(jnp.bfloat16)
        return carry

    lax.fori_loop(0, out.shape[0] // 128, make_sign, 0)

    def x_copy(ch, i, k, o):
        part = out.at[
            pl.ds(pl.multiple_of(i * tile, tile), tile),
            pl.ds(pl.multiple_of((x * chunks + ch) * lanes, lanes), lanes),
        ]
        return pltpu.make_async_remote_copy(
            src_ref=part,
            dst_ref=part,
            send_sem=x_send.at[ch, i, k],
            recv_sem=x_recv.at[ch, i, k],
            device_id={"feat": lax.rem(x + o, feat_groups)},
            device_id_type=MESH,
        )

    def h_copy(k):
        return pltpu.make_async_remote_copy(
            src_ref=edge.at[:, k * cols : (k + 1) * cols],
            dst_ref=halo,
            send_sem=h_send.at[k],
            recv_sem=h_recv.at[0],
            device_id={"atoms": z_down, "feat": k},
            device_id_type=MESH,
        )

    for ch in range(chunks):
        own_copies[ch].wait()
        for copy in z_copies[ch]:
            copy.wait_recv()

        def features(i, carry, ch=ch):
            rows = pl.ds(pl.multiple_of(i * tile, tile), tile)
            delta = jnp.dot(sign[rows, :], recv[ch], preferred_element_type=jnp.float32)
            square = delta * delta
            total = square[:, :lanes] + square[:, lanes : 2 * lanes] + square[:, 2 * lanes :]
            cols = pl.ds(pl.multiple_of((x * chunks + ch) * lanes, lanes), lanes)
            out[rows, cols] = jnp.sqrt(total + 0.01)
            for k, o in enumerate(x_steps):
                x_copy(ch, i, k, o).start()
            return carry

        lax.fori_loop(0, tiles, features, 0)
        if ch == 0:

            @pl.when(x == 0)
            def _():
                for i in range(tiles):
                    first = out[i * tile : (i + 1) * tile, :lanes]
                    edge[:, i * tile : (i + 1) * tile] = first.T[:HALO]
                for k in range(feat_groups):
                    h_copy(k).start()

    @pl.when(x == 0)
    def _():
        for k in range(feat_groups):
            h_copy(k).wait_send()

    h_copy(0).wait_recv()
    for ch in range(chunks):
        for copy in z_copies[ch]:
            copy.wait_send()

        def finish(i, carry, ch=ch):
            for k, o in enumerate(x_steps):
                x_copy(ch, i, k, o).wait()
            return carry

        lax.fori_loop(0, tiles, finish, 0)


def exchange(coords, picked, slots, room, lanes, groups, feat_groups):
    feats, width = slots.shape[0], picked.shape[1]
    chunks = coords.shape[1] // (groups * feat_groups * lanes)
    tile = min(256, feats)
    vmem = pl.BlockSpec(memory_space=pltpu.VMEM)
    z_count, x_count = max(groups - 1, 1), max(feat_groups - 1, 1)
    dma = pltpu.SemaphoreType.DMA
    return pl.pallas_call(
        functools.partial(exchange_kernel, groups, feat_groups, room, lanes, chunks, tile),
        out_shape=(
            jax.ShapeDtypeStruct((feats, feat_groups * chunks * lanes), jnp.float32),
            jax.ShapeDtypeStruct((HALO, feats // feat_groups), jnp.float32),
        ),
        in_specs=[pl.BlockSpec(memory_space=pl.ANY), vmem, vmem],
        out_specs=(vmem, vmem),
        scratch_shapes=[
            pltpu.VMEM((chunks, groups, 3, lanes, width), jnp.bfloat16),
            pltpu.VMEM((room, width), jnp.bfloat16),
            pltpu.VMEM((chunks, groups, room, 3 * lanes), jnp.bfloat16),
            pltpu.VMEM((feats, groups * room), jnp.bfloat16),
            pltpu.VMEM((chunks, groups * room, 3 * lanes), jnp.bfloat16),
            pltpu.VMEM((HALO, feats), jnp.float32),
            dma((chunks, groups)),
            dma((chunks, z_count)),
            dma((chunks, z_count)),
            dma((chunks,)),
            dma((chunks, feats // tile, x_count)),
            dma((chunks, feats // tile, x_count)),
            dma((feat_groups,)),
            dma((1,)),
        ],
        compiler_params=pltpu.CompilerParams(
            collective_id=0, has_side_effects=True, vmem_limit_bytes=48 * 1024 * 1024
        ),
    )(coords, picked, slots)


def slots_per_pass(width, refs, atoms):
    share = width * (1.0 - math.exp(-refs / atoms)) + 2.05 * math.sqrt(width)
    return min(-(-width // 16) * 16, -(-int(share) // 16) * 16)


def shards(atom_coords, atom_pairs, traj_ids):
    groups = lax.axis_size("atoms")
    feat_groups = lax.axis_size("feat")
    frames = atom_coords.shape[1]
    frames_here = frames // groups
    part = frames_here // feat_groups
    width = atom_coords.shape[3]
    cols = atom_pairs.shape[1]
    z = lax.axis_index("atoms")
    x = lax.axis_index("feat")

    pairs = lax.all_gather(atom_pairs, "feat", axis=1, tiled=True)
    feats = pairs.shape[1]
    refs = pairs.reshape(-1)
    room = slots_per_pass(width, 2 * feats, width * groups)

    atom_no = jnp.arange(groups * width, dtype=jnp.int32).reshape(groups, width)
    hit = atom_no[:, :, None] == refs[None, None, :]
    used = jnp.any(hit, axis=2)
    before = (jnp.arange(width)[:, None] < jnp.arange(width)[None, :]).astype(jnp.bfloat16)
    rank = matmul(used.astype(jnp.bfloat16), before, ((1,), (0,)))
    most = jnp.max(jnp.sum(used.astype(jnp.float32), 1))
    ref_rank = jnp.sum(jnp.where(hit, rank[:, :, None], 0.0), axis=(0, 1)).reshape(2, feats)
    ref_shard = pairs // width
    used_own = lax.dynamic_index_in_dim(used, z, 0, False)
    rank_own = lax.dynamic_index_in_dim(rank, z, 0, False)

    coords = jnp.transpose(atom_coords[0], (1, 0, 2))
    lanes = 128 if part % 128 == 0 else part
    chunks = part // lanes

    def spots(turn):
        spot = ref_rank - turn * jnp.float32(room)
        inside = (spot >= 0) & (spot < room)
        return jnp.where(inside, ref_shard * room + spot.astype(jnp.int32), -1).T

    def one_pass():
        picked = jnp.where(used_own, rank_own.astype(jnp.int32), -1)[None]
        return exchange(coords, picked, spots(jnp.float32(0.0)), room, lanes, groups, feat_groups)

    def more_passes():
        def step(carry):
            turn, delta = carry
            spot = spots(turn)
            slot = jnp.arange(room, dtype=jnp.float32) + turn * jnp.float32(room)
            pick = ((rank_own[None, :] == slot[:, None]) & used_own[None, :]).astype(jnp.bfloat16)
            grouped = coords.reshape(3, groups, feat_groups, part, width)
            blocks = lax.dynamic_index_in_dim(grouped, x, 2, False)
            chosen = matmul(pick, blocks, ((1,), (3,))).astype(jnp.bfloat16)
            chosen = jnp.transpose(chosen.reshape(room, 3, groups, chunks, lanes), (2, 3, 0, 1, 4))
            chosen = chosen.reshape(groups, chunks, room, 3 * lanes)
            got = lax.all_to_all(chosen, "atoms", split_axis=0, concat_axis=0, tiled=True)
            got = jnp.transpose(got, (0, 2, 1, 3)).reshape(groups * room, chunks * 3 * lanes)
            place = jnp.arange(groups * room, dtype=jnp.int32)
            sign = (spot[:, :1] == place).astype(jnp.bfloat16) - (spot[:, 1:] == place).astype(jnp.bfloat16)
            return turn + 1.0, delta + matmul(sign, got, ((1,), (0,)))

        _, delta = lax.while_loop(
            lambda c: c[0] * room < most,
            step,
            (jnp.float32(0.0), jnp.zeros((feats, chunks * 3 * lanes), jnp.float32)),
        )
        delta = delta.reshape(feats, chunks, 3, lanes)
        computed = jnp.sqrt(jnp.sum(delta * delta, axis=2) + 0.01).reshape(feats, part)
        both = lax.all_gather(computed, "feat", axis=1, tiled=True)
        first = lax.dynamic_slice_in_dim(both[:, :HALO], x * cols, cols, 0).T
        return both, lax.ppermute(first, "atoms", [(i, (i - 1) % groups) for i in range(groups)])

    every, incoming = lax.cond(most <= room, one_pass, more_passes)
    every = every.T
    own = lax.dynamic_slice_in_dim(every, x * cols, cols, 1)
    future = jnp.concatenate([own[LAG:], incoming[:LAG]], 0)

    ids = jnp.concatenate([traj_ids[0], jnp.full((LAG,), -1, jnp.int32)])
    ids_now = lax.dynamic_slice_in_dim(ids, z * frames_here, frames_here)
    ids_later = lax.dynamic_slice_in_dim(ids, z * frames_here + LAG, frames_here)
    valid = (ids_now == ids_later).astype(jnp.float32)[:, None]

    count_b = jnp.sum(valid)
    inverse = 1.0 / jnp.maximum(count_b, 1.0)
    now_b = jnp.sum(valid * every, 0) * inverse
    next_b = jnp.sum(valid * future, 0) * inverse
    now_c = valid * (every - now_b)
    next_c = valid * (future - next_b)
    own_c = lax.dynamic_slice_in_dim(now_c, x * cols, cols, 1)
    stats = jnp.concatenate(
        [now_b, next_b, jnp.sum(now_c * now_c, 0), jnp.sum(next_c * next_c, 0), jnp.full((128,), count_b)]
    )
    stats = lax.all_gather(stats, ("atoms", "rep"), axis=0, tiled=False)

    local = matmul(now_c, jnp.concatenate([own_c, next_c], 1), ((0,), (0,)), lax.Precision.HIGH)
    mine = lax.psum_scatter(local, ("atoms", "rep"), scatter_dimension=0, tiled=True)

    counts = stats[:, -1:]
    now_all = stats[:, :feats]
    next_all = stats[:, feats : feats + cols]
    sq_now = stats[:, feats + cols : 2 * feats + cols]
    sq_next = stats[:, 2 * feats + cols : 2 * feats + 2 * cols]
    count = jnp.sum(counts)
    mean_now = jnp.sum(counts * now_all, 0) / count
    mean_next = jnp.sum(counts * next_all, 0) / count
    off_now = now_all - mean_now
    off_next = next_all - mean_next
    spread_now = jnp.sum(sq_now + counts * off_now * off_now, 0)
    spread_next = jnp.sum(sq_next + counts * off_next * off_next, 0)
    scale_now = 1.0 / jnp.sqrt(spread_now / count + 1e-05)
    scale_next = 1.0 / jnp.sqrt(spread_next / count + 1e-05)

    rows = feats // lax.axis_size(("atoms", "rep"))
    row = lax.axis_index(("atoms", "rep")) * rows
    off_rows = lax.dynamic_slice_in_dim(off_now, row, rows, 1)
    off_cols = lax.dynamic_slice_in_dim(off_now, x * cols, cols, 1)
    mine = mine + matmul(
        counts * off_rows, jnp.concatenate([off_cols, off_next], 1), ((0,), (0,)), lax.Precision.HIGHEST
    )
    scale_rows = lax.dynamic_slice_in_dim(scale_now, row, rows)
    scale_cols = lax.dynamic_slice_in_dim(scale_now, x * cols, cols)
    mean_cols = lax.dynamic_slice_in_dim(mean_now, x * cols, cols)
    corr_inst = mine[:, :cols] / count * scale_rows[:, None] * scale_cols[None, :]
    corr_lag = mine[:, cols:] / count * scale_rows[:, None] * scale_next[None, :]
    projections = ((own - mean_cols) * scale_cols)[None]
    return (corr_inst, corr_lag, projections)


def solution(mesh):
    placed = (P(("grp", "rep"), None, None, "atoms"), P(None, "feat"), P(("grp", "rep"), None))
    return jax.shard_map(
        shards,
        mesh=mesh,
        in_specs=placed,
        out_specs=(
            P(("grp", "atoms", "rep"), "feat"),
            P(("grp", "atoms", "rep"), "feat"),
            P(("grp", "rep"), "atoms", "feat"),
        ),
        check_vma=False,
    )
```

```python
import functools
import math

import jax
import jax.numpy as jnp
from jax import lax
from jax.experimental import pallas as pl
from jax.experimental.pallas import tpu as pltpu
from jax.sharding import PartitionSpec as P

LAG = 10
HALO = 16


def matmul(left, right, dims, precision=None):
    return lax.dot_general(
        left, right, (dims, ((), ())), precision=precision, preferred_element_type=jnp.float32
    )

MESH = pl.DeviceIdType.MESH


def exchange_kernel(
    groups, feat_groups, room, lanes, chunks, tile, coords, picked, slots, out, halo, *scratch
):
    blocks, pick, chosen, sign, recv, edge, load, z_send, z_recv, z_own, x_send, x_recv, h_send, h_recv = scratch
    z, x = lax.axis_index("atoms"), lax.axis_index("feat")
    half = groups // 2
    z_steps = [half] + [o for o in range(groups - 1, 0, -1) if o != half] if groups > 1 else []
    x_steps = list(range(1, feat_groups))
    tiles = out.shape[0] // tile
    frames_here = feat_groups * chunks * lanes
    cols = halo.shape[1]
    z_dests = [lax.rem(z + o, groups) for o in z_steps] + [z]
    loads = []
    for ch in range(chunks):
        row = []
        for i, dest in enumerate(z_dests):
            start = pl.multiple_of(dest * frames_here + (x * chunks + ch) * lanes, 16)
            row.append(
                pltpu.make_async_copy(coords.at[:, pl.ds(start, lanes), :], blocks.at[ch, i], load.at[ch, i])
            )
            row[-1].start()
        loads.append(row)
    barrier = pltpu.get_barrier_semaphore()
    for o in z_steps:
        pl.semaphore_signal(barrier, 1, device_id={"atoms": lax.rem(z + o, groups)}, device_id_type=MESH)
    for o in x_steps:
        pl.semaphore_signal(barrier, 1, device_id={"feat": lax.rem(x + o, feat_groups)}, device_id_type=MESH)
    z_up, z_down = lax.rem(z + 1, groups), lax.rem(z + groups - 1, groups)

    @pl.when(x == 0)
    def _():
        for k in x_steps:
            pl.semaphore_signal(barrier, 1, device_id={"atoms": z_down, "feat": k}, device_id_type=MESH)

    @pl.when(x != 0)
    def _():
        pl.semaphore_signal(barrier, 1, device_id={"atoms": z_up, "feat": 0}, device_id_type=MESH)

    width = picked.shape[1]
    slot_no = lax.broadcasted_iota(jnp.int32, (room, width), 0)
    pick[...] = jnp.where(slot_no == picked[...], 1.0, 0.0).astype(jnp.bfloat16)

    @pl.when(x == 0)
    def _():
        pl.semaphore_wait(barrier, len(z_steps) + 2 * len(x_steps))

    @pl.when(x != 0)
    def _():
        pl.semaphore_wait(barrier, len(z_steps) + len(x_steps) + 1)

    def fill(ch, i):
        loads[ch][i].wait()
        for c in range(3):
            got = lax.dot_general(
                pick[...], blocks[ch, i, c], (((1,), (1,)), ((), ())), preferred_element_type=jnp.float32
            )
            chosen[ch, i, :, c * lanes : (c + 1) * lanes] = got.astype(jnp.bfloat16)

    here = pl.ds(pl.multiple_of(z * room, 16), room)
    z_copies = []
    for ch in range(chunks):
        row = []
        for i, o in enumerate(z_steps):
            fill(ch, i)
            row.append(
                pltpu.make_async_remote_copy(
                    src_ref=chosen.at[ch, i],
                    dst_ref=recv.at[ch, here],
                    send_sem=z_send.at[ch, i],
                    recv_sem=z_recv.at[ch, i],
                    device_id={"atoms": z_dests[i]},
                    device_id_type=MESH,
                )
            )
            row[-1].start()
        z_copies.append(row)
    own_copies = []
    for ch in range(chunks):
        fill(ch, len(z_steps))
        own_copies.append(
            pltpu.make_async_copy(chosen.at[ch, len(z_steps)], recv.at[ch, here], z_own.at[ch])
        )
        own_copies[-1].start()

    place = lax.broadcasted_iota(jnp.int32, (128, groups * room), 1)

    def make_sign(i, carry):
        rows = pl.ds(pl.multiple_of(i * 128, 128), 128)
        pair = slots[rows, :]
        value = jnp.where(place == pair[:, 0:1], 1.0, 0.0) - jnp.where(place == pair[:, 1:2], 1.0, 0.0)
        sign[rows, :] = value.astype(jnp.bfloat16)
        return carry

    lax.fori_loop(0, out.shape[0] // 128, make_sign, 0)

    def x_copy(ch, i, k, o):
        part = out.at[
            pl.ds(pl.multiple_of(i * tile, tile), tile),
            pl.ds(pl.multiple_of((x * chunks + ch) * lanes, lanes), lanes),
        ]
        return pltpu.make_async_remote_copy(
            src_ref=part,
            dst_ref=part,
            send_sem=x_send.at[ch, i, k],
            recv_sem=x_recv.at[ch, i, k],
            device_id={"feat": lax.rem(x + o, feat_groups)},
            device_id_type=MESH,
        )

    def h_copy(k):
        return pltpu.make_async_remote_copy(
            src_ref=edge.at[:, k * cols : (k + 1) * cols],
            dst_ref=halo,
            send_sem=h_send.at[k],
            recv_sem=h_recv.at[0],
            device_id={"atoms": z_down, "feat": k},
            device_id_type=MESH,
        )

    for ch in range(chunks):
        own_copies[ch].wait()
        for copy in z_copies[ch]:
            copy.wait_recv()

        def features(i, carry, ch=ch):
            rows = pl.ds(pl.multiple_of(i * tile, tile), tile)
            delta = jnp.dot(sign[rows, :], recv[ch], preferred_element_type=jnp.float32)
            square = delta * delta
            total = square[:, :lanes] + square[:, lanes : 2 * lanes] + square[:, 2 * lanes :]
            cols = pl.ds(pl.multiple_of((x * chunks + ch) * lanes, lanes), lanes)
            out[rows, cols] = jnp.sqrt(total + 0.01)
            for k, o in enumerate(x_steps):
                x_copy(ch, i, k, o).start()
            return carry

        lax.fori_loop(0, tiles, features, 0)
        if ch == 0:

            @pl.when(x == 0)
            def _():
                for i in range(tiles):
                    first = out[i * tile : (i + 1) * tile, :lanes]
                    edge[:, i * tile : (i + 1) * tile] = first.T[:HALO]
                for k in range(feat_groups):
                    h_copy(k).start()

    @pl.when(x == 0)
    def _():
        for k in range(feat_groups):
            h_copy(k).wait_send()

    h_copy(0).wait_recv()
    for ch in range(chunks):
        for copy in z_copies[ch]:
            copy.wait_send()

        def finish(i, carry, ch=ch):
            for k, o in enumerate(x_steps):
                x_copy(ch, i, k, o).wait()
            return carry

        lax.fori_loop(0, tiles, finish, 0)


def exchange(coords, picked, slots, room, lanes, groups, feat_groups):
    feats, width = slots.shape[0], picked.shape[1]
    chunks = coords.shape[1] // (groups * feat_groups * lanes)
    tile = min(256, feats)
    vmem = pl.BlockSpec(memory_space=pltpu.VMEM)
    z_count, x_count = max(groups - 1, 1), max(feat_groups - 1, 1)
    dma = pltpu.SemaphoreType.DMA
    return pl.pallas_call(
        functools.partial(exchange_kernel, groups, feat_groups, room, lanes, chunks, tile),
        out_shape=(
            jax.ShapeDtypeStruct((feats, feat_groups * chunks * lanes), jnp.float32),
            jax.ShapeDtypeStruct((HALO, feats // feat_groups), jnp.float32),
        ),
        in_specs=[pl.BlockSpec(memory_space=pl.ANY), vmem, vmem],
        out_specs=(vmem, vmem),
        scratch_shapes=[
            pltpu.VMEM((chunks, groups, 3, lanes, width), jnp.bfloat16),
            pltpu.VMEM((room, width), jnp.bfloat16),
            pltpu.VMEM((chunks, groups, room, 3 * lanes), jnp.bfloat16),
            pltpu.VMEM((feats, groups * room), jnp.bfloat16),
            pltpu.VMEM((chunks, groups * room, 3 * lanes), jnp.bfloat16),
            pltpu.VMEM((HALO, feats), jnp.float32),
            dma((chunks, groups)),
            dma((chunks, z_count)),
            dma((chunks, z_count)),
            dma((chunks,)),
            dma((chunks, feats // tile, x_count)),
            dma((chunks, feats // tile, x_count)),
            dma((feat_groups,)),
            dma((1,)),
        ],
        compiler_params=pltpu.CompilerParams(
            collective_id=0, has_side_effects=True, vmem_limit_bytes=48 * 1024 * 1024
        ),
    )(coords, picked, slots)


def reduce_kernel(groups, reps, local, stats, out, gathered, core, sums, left, right, *sems):
    c_send, c_recv, s_own, s_send, s_recv, z_send, l_recv, r_recv = sems
    z, r = lax.axis_index("atoms"), lax.axis_index("rep")
    peers = [(a, b) for a in range(groups) for b in range(reps) if (a, b) != (0, 0)]
    barrier = pltpu.get_barrier_semaphore()

    def peer(a, b):
        return {"atoms": lax.rem(z + a, groups), "rep": lax.rem(r + b, reps)}

    for a, b in peers:
        pl.semaphore_signal(barrier, 1, device_id=peer(a, b), device_id_type=MESH)
    pl.semaphore_wait(barrier, len(peers))

    order = []
    for k in range((groups + 1) // 2):
        order += [groups - 1 - k] + ([k] if k != groups - 1 - k else [])
    core_copies = {}
    for d in order:
        for b in range(1, reps):
            core_copies[d, b] = pltpu.make_async_remote_copy(
                src_ref=local.at[d, lax.rem(r + b, reps)],
                dst_ref=core.at[b - 1, d],
                send_sem=c_send.at[b - 1, d],
                recv_sem=c_recv.at[b - 1, d],
                device_id={"rep": lax.rem(r + b, reps)},
                device_id_type=MESH,
            )
            core_copies[d, b].start()
    me = z * reps + r
    own = pltpu.make_async_copy(stats, gathered.at[me], s_own.at[0])
    own.start()
    stat_copies = []
    for k, (a, b) in enumerate(peers):
        stat_copies.append(
            pltpu.make_async_remote_copy(
                src_ref=stats,
                dst_ref=gathered.at[me],
                send_sem=s_send.at[k],
                recv_sem=s_recv.at[k],
                device_id=peer(a, b),
                device_id_type=MESH,
            )
        )
        stat_copies[-1].start()


    def hop(d, step):
        return pltpu.make_async_remote_copy(
            src_ref=sums.at[d],
            dst_ref=(left if step > 0 else right).at[d],
            send_sem=z_send.at[d],
            recv_sem=(l_recv if step > 0 else r_recv).at[d],
            device_id={"atoms": lax.rem(z + step + groups, groups)},
            device_id_type=MESH,
        )

    for d in order:
        total = local[d, r]
        for b in range(1, reps):
            core_copies[d, b].wait_recv()
            total = total + core[b - 1, d]
        sums[d] = total

        if d > 0:

            @pl.when(z == 0)
            def _(d=d):
                hop(d, 1).start()

        if d < groups - 1:

            @pl.when(z == groups - 1)
            def _(d=d):
                hop(d, -1).start()

    for k in range(groups):
        up, down = groups - 1 - k, k

        @pl.when((z > 0) & (z < up))
        def _(d=up):
            hop(d, 1).wait_recv()
            sums[d] = sums[d] + left[d]
            hop(d, 1).start()

        @pl.when((z < groups - 1) & (z > down))
        def _(d=down):
            hop(d, -1).wait_recv()
            sums[d] = sums[d] + right[d]
            hop(d, -1).start()

    for d in range(groups):

        @pl.when(z == d)
        def _(d=d):
            total = sums[d]
            if d > 0:
                hop(d, 1).wait_recv()
                total = total + left[d]
            if d < groups - 1:
                hop(d, -1).wait_recv()
                total = total + right[d]
            out[...] = total

        @pl.when(z < d)
        def _(d=d):
            hop(d, 1).wait_send()

        @pl.when(z > d)
        def _(d=d):
            hop(d, -1).wait_send()

    for copy in core_copies.values():
        copy.wait_send()
    own.wait()
    for copy in stat_copies:
        copy.wait()


def reduce_blocks(local, stats, groups, reps):
    rows, width = local.shape[0] // (groups * reps), local.shape[1]
    vmem = pl.BlockSpec(memory_space=pltpu.VMEM)
    dma = pltpu.SemaphoreType.DMA
    block = pltpu.VMEM((groups, rows, width), jnp.float32)
    others = max(groups * reps - 1, 1)
    others_core = max(reps - 1, 1)
    return pl.pallas_call(
        functools.partial(reduce_kernel, groups, reps),
        out_shape=(
            jax.ShapeDtypeStruct((rows, width), jnp.float32),
            jax.ShapeDtypeStruct((groups * reps,) + stats.shape, jnp.float32),
        ),
        in_specs=[vmem, vmem],
        out_specs=(vmem, vmem),
        scratch_shapes=[
            pltpu.VMEM((others_core, groups, rows, width), jnp.float32),
            block,
            block,
            block,
            dma((others_core, groups)),
            dma((others_core, groups)),
            dma((1,)),
            dma((others,)),
            dma((others,)),
            dma((groups,)),
            dma((groups,)),
            dma((groups,)),
        ],
        compiler_params=pltpu.CompilerParams(
            collective_id=1, has_side_effects=True, vmem_limit_bytes=48 * 1024 * 1024
        ),
    )(local.reshape(groups, reps, rows, width), stats)


def slots_per_pass(width, refs, atoms):
    share = width * (1.0 - math.exp(-refs / atoms)) + 2.05 * math.sqrt(width)
    return min(-(-width // 16) * 16, -(-int(share) // 16) * 16)


def shards(atom_coords, atom_pairs, traj_ids):
    groups = lax.axis_size("atoms")
    feat_groups = lax.axis_size("feat")
    frames = atom_coords.shape[1]
    frames_here = frames // groups
    part = frames_here // feat_groups
    width = atom_coords.shape[3]
    cols = atom_pairs.shape[1]
    z = lax.axis_index("atoms")
    x = lax.axis_index("feat")

    pairs = lax.all_gather(atom_pairs, "feat", axis=1, tiled=True)
    feats = pairs.shape[1]
    refs = pairs.reshape(-1)
    room = slots_per_pass(width, 2 * feats, width * groups)

    atom_no = jnp.arange(groups * width, dtype=jnp.int32).reshape(groups, width)
    hit = atom_no[:, :, None] == refs[None, None, :]
    used = jnp.any(hit, axis=2)
    before = (jnp.arange(width)[:, None] < jnp.arange(width)[None, :]).astype(jnp.bfloat16)
    rank = matmul(used.astype(jnp.bfloat16), before, ((1,), (0,)))
    most = jnp.max(jnp.sum(used.astype(jnp.float32), 1))
    ref_rank = jnp.sum(jnp.where(hit, rank[:, :, None], 0.0), axis=(0, 1)).reshape(2, feats)
    ref_shard = pairs // width
    used_own = lax.dynamic_index_in_dim(used, z, 0, False)
    rank_own = lax.dynamic_index_in_dim(rank, z, 0, False)

    coords = jnp.transpose(atom_coords[0], (1, 0, 2))
    lanes = 128 if part % 128 == 0 else part
    chunks = part // lanes

    def spots(turn):
        spot = ref_rank - turn * jnp.float32(room)
        inside = (spot >= 0) & (spot < room)
        return jnp.where(inside, ref_shard * room + spot.astype(jnp.int32), -1).T

    def one_pass():
        picked = jnp.where(used_own, rank_own.astype(jnp.int32), -1)[None]
        return exchange(coords, picked, spots(jnp.float32(0.0)), room, lanes, groups, feat_groups)

    def more_passes():
        def step(carry):
            turn, delta = carry
            spot = spots(turn)
            slot = jnp.arange(room, dtype=jnp.float32) + turn * jnp.float32(room)
            pick = ((rank_own[None, :] == slot[:, None]) & used_own[None, :]).astype(jnp.bfloat16)
            grouped = coords.reshape(3, groups, feat_groups, part, width)
            blocks = lax.dynamic_index_in_dim(grouped, x, 2, False)
            chosen = matmul(pick, blocks, ((1,), (3,))).astype(jnp.bfloat16)
            chosen = jnp.transpose(chosen.reshape(room, 3, groups, chunks, lanes), (2, 3, 0, 1, 4))
            chosen = chosen.reshape(groups, chunks, room, 3 * lanes)
            got = lax.all_to_all(chosen, "atoms", split_axis=0, concat_axis=0, tiled=True)
            got = jnp.transpose(got, (0, 2, 1, 3)).reshape(groups * room, chunks * 3 * lanes)
            place = jnp.arange(groups * room, dtype=jnp.int32)
            sign = (spot[:, :1] == place).astype(jnp.bfloat16) - (spot[:, 1:] == place).astype(jnp.bfloat16)
            return turn + 1.0, delta + matmul(sign, got, ((1,), (0,)))

        _, delta = lax.while_loop(
            lambda c: c[0] * room < most,
            step,
            (jnp.float32(0.0), jnp.zeros((feats, chunks * 3 * lanes), jnp.float32)),
        )
        delta = delta.reshape(feats, chunks, 3, lanes)
        computed = jnp.sqrt(jnp.sum(delta * delta, axis=2) + 0.01).reshape(feats, part)
        both = jnp.zeros((feats, frames_here), jnp.float32)
        for o in range(feat_groups):
            turned = lax.ppermute(computed, "feat", [(i, (i + o) % feat_groups) for i in range(feat_groups)])
            both = lax.dynamic_update_slice_in_dim(both, turned, ((x - o) % feat_groups) * part, 1)
        first = lax.dynamic_slice_in_dim(both[:, :HALO], x * cols, cols, 0).T
        return both, lax.ppermute(first, "atoms", [(i, (i - 1) % groups) for i in range(groups)])

    every, incoming = lax.cond(most <= room, one_pass, more_passes)
    every = every.T
    own = lax.dynamic_slice_in_dim(every, x * cols, cols, 1)
    future = jnp.concatenate([own[LAG:], incoming[:LAG]], 0)

    ids = jnp.concatenate([traj_ids[0], jnp.full((LAG,), -1, jnp.int32)])
    ids_now = lax.dynamic_slice_in_dim(ids, z * frames_here, frames_here)
    ids_later = lax.dynamic_slice_in_dim(ids, z * frames_here + LAG, frames_here)
    valid = (ids_now == ids_later).astype(jnp.float32)[:, None]

    count_b = jnp.sum(valid)
    inverse = 1.0 / jnp.maximum(count_b, 1.0)
    now_b = jnp.sum(valid * every, 0) * inverse
    next_b = jnp.sum(valid * future, 0) * inverse
    now_c = valid * (every - now_b)
    next_c = valid * (future - next_b)
    own_c = lax.dynamic_slice_in_dim(now_c, x * cols, cols, 1)
    stats = jnp.concatenate(
        [now_b, next_b, jnp.sum(now_c * now_c, 0), jnp.sum(next_c * next_c, 0), jnp.full((128,), count_b)]
    )
    reps = lax.axis_size("rep")
    stats = jnp.pad(stats, (0, -stats.shape[0] % 1024)).reshape(-1, 128)
    local = matmul(now_c, jnp.concatenate([own_c, next_c], 1), ((0,), (0,)), lax.Precision.HIGH)
    mine, stats = reduce_blocks(local, stats, groups, reps)
    stats = stats.reshape(groups * reps, -1)

    counts = stats[:, 2 * feats + 2 * cols :][:, :1]
    now_all = stats[:, :feats]
    next_all = stats[:, feats : feats + cols]
    sq_now = stats[:, feats + cols : 2 * feats + cols]
    sq_next = stats[:, 2 * feats + cols : 2 * feats + 2 * cols]
    count = jnp.sum(counts)
    mean_now = jnp.sum(counts * now_all, 0) / count
    mean_next = jnp.sum(counts * next_all, 0) / count
    off_now = now_all - mean_now
    off_next = next_all - mean_next
    spread_now = jnp.sum(sq_now + counts * off_now * off_now, 0)
    spread_next = jnp.sum(sq_next + counts * off_next * off_next, 0)
    scale_now = 1.0 / jnp.sqrt(spread_now / count + 1e-05)
    scale_next = 1.0 / jnp.sqrt(spread_next / count + 1e-05)

    rows = feats // lax.axis_size(("atoms", "rep"))
    row = lax.axis_index(("atoms", "rep")) * rows
    off_rows = lax.dynamic_slice_in_dim(off_now, row, rows, 1)
    off_cols = lax.dynamic_slice_in_dim(off_now, x * cols, cols, 1)
    mine = mine + matmul(
        counts * off_rows, jnp.concatenate([off_cols, off_next], 1), ((0,), (0,)), lax.Precision.HIGHEST
    )
    scale_rows = lax.dynamic_slice_in_dim(scale_now, row, rows)
    scale_cols = lax.dynamic_slice_in_dim(scale_now, x * cols, cols)
    mean_cols = lax.dynamic_slice_in_dim(mean_now, x * cols, cols)
    corr_inst = mine[:, :cols] / count * scale_rows[:, None] * scale_cols[None, :]
    corr_lag = mine[:, cols:] / count * scale_rows[:, None] * scale_next[None, :]
    projections = ((own - mean_cols) * scale_cols)[None]
    return (corr_inst, corr_lag, projections)


def solution(mesh):
    placed = (P(("grp", "rep"), None, None, "atoms"), P(None, "feat"), P(("grp", "rep"), None))
    return jax.shard_map(
        shards,
        mesh=mesh,
        in_specs=placed,
        out_specs=(
            P(("grp", "atoms", "rep"), "feat"),
            P(("grp", "atoms", "rep"), "feat"),
            P(("grp", "rep"), "atoms", "feat"),
        ),
        check_vma=False,
    )
```

```python
import functools
import math

import jax
import jax.numpy as jnp
from jax import lax
from jax.experimental import pallas as pl
from jax.experimental.pallas import tpu as pltpu
from jax.sharding import PartitionSpec as P

LAG = 10
HALO = 16


def matmul(left, right, dims, precision=None):
    return lax.dot_general(
        left, right, (dims, ((), ())), precision=precision, preferred_element_type=jnp.float32
    )

MESH = pl.DeviceIdType.MESH


def exchange_kernel(
    groups, feat_groups, room, lanes, chunks, tile, coords, picked, slots, out, halo, *scratch
):
    blocks, pick, chosen, sign, recv, edge, load, z_send, z_recv, z_own, x_send, x_recv, h_send, h_recv = scratch
    z, x = lax.axis_index("atoms"), lax.axis_index("feat")
    half = groups // 2
    z_steps = [half] + [o for o in range(groups - 1, 0, -1) if o != half] if groups > 1 else []
    x_steps = list(range(1, feat_groups))
    tiles = out.shape[0] // tile
    frames_here = feat_groups * chunks * lanes
    cols = halo.shape[1]
    z_dests = [lax.rem(z + o, groups) for o in z_steps] + [z]
    loads = []
    for ch in range(chunks):
        row = []
        for i, dest in enumerate(z_dests):
            start = pl.multiple_of(dest * frames_here + (x * chunks + ch) * lanes, 16)
            row.append(
                pltpu.make_async_copy(coords.at[:, pl.ds(start, lanes), :], blocks.at[ch, i], load.at[ch, i])
            )
            row[-1].start()
        loads.append(row)
    barrier = pltpu.get_barrier_semaphore()
    for o in z_steps:
        pl.semaphore_signal(barrier, 1, device_id={"atoms": lax.rem(z + o, groups)}, device_id_type=MESH)
    for o in x_steps:
        pl.semaphore_signal(barrier, 1, device_id={"feat": lax.rem(x + o, feat_groups)}, device_id_type=MESH)
    z_up, z_down = lax.rem(z + 1, groups), lax.rem(z + groups - 1, groups)

    @pl.when(x == 0)
    def _():
        for k in x_steps:
            pl.semaphore_signal(barrier, 1, device_id={"atoms": z_down, "feat": k}, device_id_type=MESH)

    @pl.when(x != 0)
    def _():
        pl.semaphore_signal(barrier, 1, device_id={"atoms": z_up, "feat": 0}, device_id_type=MESH)

    width = picked.shape[1]
    slot_no = lax.broadcasted_iota(jnp.int32, (room, width), 0)
    pick[...] = jnp.where(slot_no == picked[...], 1.0, 0.0).astype(jnp.bfloat16)

    @pl.when(x == 0)
    def _():
        pl.semaphore_wait(barrier, len(z_steps) + 2 * len(x_steps))

    @pl.when(x != 0)
    def _():
        pl.semaphore_wait(barrier, len(z_steps) + len(x_steps) + 1)

    def fill(ch, i):
        loads[ch][i].wait()
        for c in range(3):
            got = lax.dot_general(
                pick[...], blocks[ch, i, c], (((1,), (1,)), ((), ())), preferred_element_type=jnp.float32
            )
            chosen[ch, i, :, c * lanes : (c + 1) * lanes] = got.astype(jnp.bfloat16)

    here = pl.ds(pl.multiple_of(z * room, 16), room)
    z_copies = []
    for ch in range(chunks):
        row = []
        for i, o in enumerate(z_steps):
            fill(ch, i)
            row.append(
                pltpu.make_async_remote_copy(
                    src_ref=chosen.at[ch, i],
                    dst_ref=recv.at[ch, here],
                    send_sem=z_send.at[ch, i],
                    recv_sem=z_recv.at[ch, i],
                    device_id={"atoms": z_dests[i]},
                    device_id_type=MESH,
                )
            )
            row[-1].start()
        z_copies.append(row)
    own_copies = []
    for ch in range(chunks):
        fill(ch, len(z_steps))
        own_copies.append(
            pltpu.make_async_copy(chosen.at[ch, len(z_steps)], recv.at[ch, here], z_own.at[ch])
        )
        own_copies[-1].start()

    place = lax.broadcasted_iota(jnp.int32, (128, groups * room), 1)

    def make_sign(i, carry):
        rows = pl.ds(pl.multiple_of(i * 128, 128), 128)
        pair = slots[rows, :]
        value = jnp.where(place == pair[:, 0:1], 1.0, 0.0) - jnp.where(place == pair[:, 1:2], 1.0, 0.0)
        sign[rows, :] = value.astype(jnp.bfloat16)
        return carry

    lax.fori_loop(0, out.shape[0] // 128, make_sign, 0)

    def x_copy(ch, i, k, o):
        part = out.at[
            pl.ds(pl.multiple_of(i * tile, tile), tile),
            pl.ds(pl.multiple_of((x * chunks + ch) * lanes, lanes), lanes),
        ]
        return pltpu.make_async_remote_copy(
            src_ref=part,
            dst_ref=part,
            send_sem=x_send.at[ch, i, k],
            recv_sem=x_recv.at[ch, i, k],
            device_id={"feat": lax.rem(x + o, feat_groups)},
            device_id_type=MESH,
        )

    def h_copy(k):
        return pltpu.make_async_remote_copy(
            src_ref=edge.at[:, k * cols : (k + 1) * cols],
            dst_ref=halo,
            send_sem=h_send.at[k],
            recv_sem=h_recv.at[0],
            device_id={"atoms": z_down, "feat": k},
            device_id_type=MESH,
        )

    for ch in range(chunks):
        own_copies[ch].wait()
        for copy in z_copies[ch]:
            copy.wait_recv()

        def features(i, carry, ch=ch):
            rows = pl.ds(pl.multiple_of(i * tile, tile), tile)
            delta = jnp.dot(sign[rows, :], recv[ch], preferred_element_type=jnp.float32)
            square = delta * delta
            total = square[:, :lanes] + square[:, lanes : 2 * lanes] + square[:, 2 * lanes :]
            cols = pl.ds(pl.multiple_of((x * chunks + ch) * lanes, lanes), lanes)
            out[rows, cols] = jnp.sqrt(total + 0.01)
            for k, o in enumerate(x_steps):
                x_copy(ch, i, k, o).start()
            return carry

        lax.fori_loop(0, tiles, features, 0)
        if ch == 0:

            @pl.when(x == 0)
            def _():
                for i in range(tiles):
                    first = out[i * tile : (i + 1) * tile, :lanes]
                    edge[:, i * tile : (i + 1) * tile] = first.T[:HALO]
                for k in range(feat_groups):
                    h_copy(k).start()

    @pl.when(x == 0)
    def _():
        for k in range(feat_groups):
            h_copy(k).wait_send()

    h_copy(0).wait_recv()
    for ch in range(chunks):
        for copy in z_copies[ch]:
            copy.wait_send()

        def finish(i, carry, ch=ch):
            for k, o in enumerate(x_steps):
                x_copy(ch, i, k, o).wait()
            return carry

        lax.fori_loop(0, tiles, finish, 0)


def exchange(coords, picked, slots, room, lanes, groups, feat_groups):
    feats, width = slots.shape[0], picked.shape[1]
    chunks = coords.shape[1] // (groups * feat_groups * lanes)
    tile = min(256, feats)
    vmem = pl.BlockSpec(memory_space=pltpu.VMEM)
    z_count, x_count = max(groups - 1, 1), max(feat_groups - 1, 1)
    dma = pltpu.SemaphoreType.DMA
    return pl.pallas_call(
        functools.partial(exchange_kernel, groups, feat_groups, room, lanes, chunks, tile),
        out_shape=(
            jax.ShapeDtypeStruct((feats, feat_groups * chunks * lanes), jnp.float32),
            jax.ShapeDtypeStruct((HALO, feats // feat_groups), jnp.float32),
        ),
        in_specs=[pl.BlockSpec(memory_space=pl.ANY), vmem, vmem],
        out_specs=(vmem, vmem),
        scratch_shapes=[
            pltpu.VMEM((chunks, groups, 3, lanes, width), jnp.bfloat16),
            pltpu.VMEM((room, width), jnp.bfloat16),
            pltpu.VMEM((chunks, groups, room, 3 * lanes), jnp.bfloat16),
            pltpu.VMEM((feats, groups * room), jnp.bfloat16),
            pltpu.VMEM((chunks, groups * room, 3 * lanes), jnp.bfloat16),
            pltpu.VMEM((HALO, feats), jnp.float32),
            dma((chunks, groups)),
            dma((chunks, z_count)),
            dma((chunks, z_count)),
            dma((chunks,)),
            dma((chunks, feats // tile, x_count)),
            dma((chunks, feats // tile, x_count)),
            dma((feat_groups,)),
            dma((1,)),
        ],
        compiler_params=pltpu.CompilerParams(
            collective_id=0, has_side_effects=True, vmem_limit_bytes=48 * 1024 * 1024
        ),
    )(coords, picked, slots)


def reduce_kernel(groups, reps, local, stats, out, gathered, core, sums, left, right, *sems):
    c_send, c_recv, s_own, s_send, s_recv, z_send, l_recv, r_recv = sems
    z, r = lax.axis_index("atoms"), lax.axis_index("rep")
    peers = [(a, b) for a in range(groups) for b in range(reps) if (a, b) != (0, 0)]
    barrier = pltpu.get_barrier_semaphore()

    def peer(a, b):
        return {"atoms": lax.rem(z + a, groups), "rep": lax.rem(r + b, reps)}

    for a, b in peers:
        pl.semaphore_signal(barrier, 1, device_id=peer(a, b), device_id_type=MESH)
    pl.semaphore_wait(barrier, len(peers))

    order = []
    for k in range((groups + 1) // 2):
        order += [groups - 1 - k] + ([k] if k != groups - 1 - k else [])
    core_copies = {}
    for d in order:
        for b in range(1, reps):
            core_copies[d, b] = pltpu.make_async_remote_copy(
                src_ref=local.at[d, lax.rem(r + b, reps)],
                dst_ref=core.at[b - 1, d],
                send_sem=c_send.at[b - 1, d],
                recv_sem=c_recv.at[b - 1, d],
                device_id={"rep": lax.rem(r + b, reps)},
                device_id_type=MESH,
            )
            core_copies[d, b].start()
    me = z * reps + r
    own = pltpu.make_async_copy(stats, gathered.at[me], s_own.at[0])
    own.start()
    stat_copies = []
    for k, (a, b) in enumerate(peers):
        stat_copies.append(
            pltpu.make_async_remote_copy(
                src_ref=stats,
                dst_ref=gathered.at[me],
                send_sem=s_send.at[k],
                recv_sem=s_recv.at[k],
                device_id=peer(a, b),
                device_id_type=MESH,
            )
        )
        stat_copies[-1].start()


    def hop(d, step):
        return pltpu.make_async_remote_copy(
            src_ref=sums.at[d],
            dst_ref=(left if step > 0 else right).at[d],
            send_sem=z_send.at[d],
            recv_sem=(l_recv if step > 0 else r_recv).at[d],
            device_id={"atoms": lax.rem(z + step + groups, groups)},
            device_id_type=MESH,
        )

    ready, sent = set(), 0
    for d in order:
        total = local[d, r]
        for b in range(1, reps):
            core_copies[d, b].wait_recv()
            total = total + core[b - 1, d]
        sums[d] = total

        if d > 0:

            @pl.when(z == 0)
            def _(d=d):
                hop(d, 1).start()

        ready.add(d)
        while sent < groups - 1 and sent in ready:

            @pl.when(z == groups - 1)
            def _(d=sent):
                hop(d, -1).start()

            sent += 1

    for k in range(groups):
        up, down = groups - 1 - k, k

        @pl.when((z > 0) & (z < up))
        def _(d=up):
            hop(d, 1).wait_recv()
            sums[d] = sums[d] + left[d]
            hop(d, 1).start()

        @pl.when((z < groups - 1) & (z > down))
        def _(d=down):
            hop(d, -1).wait_recv()
            sums[d] = sums[d] + right[d]
            hop(d, -1).start()

    for d in range(groups):

        @pl.when(z == d)
        def _(d=d):
            total = sums[d]
            if d > 0:
                hop(d, 1).wait_recv()
                total = total + left[d]
            if d < groups - 1:
                hop(d, -1).wait_recv()
                total = total + right[d]
            out[...] = total

        @pl.when(z < d)
        def _(d=d):
            hop(d, 1).wait_send()

        @pl.when(z > d)
        def _(d=d):
            hop(d, -1).wait_send()

    for copy in core_copies.values():
        copy.wait_send()
    own.wait()
    for copy in stat_copies:
        copy.wait()


def reduce_blocks(local, stats, groups, reps):
    rows, width = local.shape[0] // (groups * reps), local.shape[1]
    vmem = pl.BlockSpec(memory_space=pltpu.VMEM)
    dma = pltpu.SemaphoreType.DMA
    block = pltpu.VMEM((groups, rows, width), jnp.float32)
    others = max(groups * reps - 1, 1)
    others_core = max(reps - 1, 1)
    return pl.pallas_call(
        functools.partial(reduce_kernel, groups, reps),
        out_shape=(
            jax.ShapeDtypeStruct((rows, width), jnp.float32),
            jax.ShapeDtypeStruct((groups * reps,) + stats.shape, jnp.float32),
        ),
        in_specs=[vmem, vmem],
        out_specs=(vmem, vmem),
        scratch_shapes=[
            pltpu.VMEM((others_core, groups, rows, width), jnp.float32),
            block,
            block,
            block,
            dma((others_core, groups)),
            dma((others_core, groups)),
            dma((1,)),
            dma((others,)),
            dma((others,)),
            dma((groups,)),
            dma((groups,)),
            dma((groups,)),
        ],
        compiler_params=pltpu.CompilerParams(
            collective_id=1, has_side_effects=True, vmem_limit_bytes=48 * 1024 * 1024
        ),
    )(local.reshape(groups, reps, rows, width), stats)


def slots_per_pass(width, refs, atoms):
    share = width * (1.0 - math.exp(-refs / atoms)) + 2.05 * math.sqrt(width)
    return min(-(-width // 16) * 16, -(-int(share) // 16) * 16)


def shards(atom_coords, atom_pairs, traj_ids):
    groups = lax.axis_size("atoms")
    feat_groups = lax.axis_size("feat")
    frames = atom_coords.shape[1]
    frames_here = frames // groups
    part = frames_here // feat_groups
    width = atom_coords.shape[3]
    cols = atom_pairs.shape[1]
    z = lax.axis_index("atoms")
    x = lax.axis_index("feat")

    pairs = lax.all_gather(atom_pairs, "feat", axis=1, tiled=True)
    feats = pairs.shape[1]
    refs = pairs.reshape(-1)
    room = slots_per_pass(width, 2 * feats, width * groups)

    atom_no = jnp.arange(groups * width, dtype=jnp.int32).reshape(groups, width)
    hit = atom_no[:, :, None] == refs[None, None, :]
    used = jnp.any(hit, axis=2)
    before = (jnp.arange(width)[:, None] < jnp.arange(width)[None, :]).astype(jnp.bfloat16)
    rank = matmul(used.astype(jnp.bfloat16), before, ((1,), (0,)))
    most = jnp.max(jnp.sum(used.astype(jnp.float32), 1))
    ref_rank = jnp.sum(jnp.where(hit, rank[:, :, None], 0.0), axis=(0, 1)).reshape(2, feats)
    ref_shard = pairs // width
    used_own = lax.dynamic_index_in_dim(used, z, 0, False)
    rank_own = lax.dynamic_index_in_dim(rank, z, 0, False)

    coords = jnp.transpose(atom_coords[0], (1, 0, 2))
    lanes = 128 if part % 128 == 0 else part
    chunks = part // lanes

    def spots(turn):
        spot = ref_rank - turn * jnp.float32(room)
        inside = (spot >= 0) & (spot < room)
        return jnp.where(inside, ref_shard * room + spot.astype(jnp.int32), -1).T

    def one_pass():
        picked = jnp.where(used_own, rank_own.astype(jnp.int32), -1)[None]
        return exchange(coords, picked, spots(jnp.float32(0.0)), room, lanes, groups, feat_groups)

    def more_passes():
        def step(carry):
            turn, delta = carry
            spot = spots(turn)
            slot = jnp.arange(room, dtype=jnp.float32) + turn * jnp.float32(room)
            pick = ((rank_own[None, :] == slot[:, None]) & used_own[None, :]).astype(jnp.bfloat16)
            grouped = coords.reshape(3, groups, feat_groups, part, width)
            blocks = lax.dynamic_index_in_dim(grouped, x, 2, False)
            chosen = matmul(pick, blocks, ((1,), (3,))).astype(jnp.bfloat16)
            chosen = jnp.transpose(chosen.reshape(room, 3, groups, chunks, lanes), (2, 3, 0, 1, 4))
            chosen = chosen.reshape(groups, chunks, room, 3 * lanes)
            got = lax.all_to_all(chosen, "atoms", split_axis=0, concat_axis=0, tiled=True)
            got = jnp.transpose(got, (0, 2, 1, 3)).reshape(groups * room, chunks * 3 * lanes)
            place = jnp.arange(groups * room, dtype=jnp.int32)
            sign = (spot[:, :1] == place).astype(jnp.bfloat16) - (spot[:, 1:] == place).astype(jnp.bfloat16)
            return turn + 1.0, delta + matmul(sign, got, ((1,), (0,)))

        _, delta = lax.while_loop(
            lambda c: c[0] * room < most,
            step,
            (jnp.float32(0.0), jnp.zeros((feats, chunks * 3 * lanes), jnp.float32)),
        )
        delta = delta.reshape(feats, chunks, 3, lanes)
        computed = jnp.sqrt(jnp.sum(delta * delta, axis=2) + 0.01).reshape(feats, part)
        both = jnp.zeros((feats, frames_here), jnp.float32)
        for o in range(feat_groups):
            turned = lax.ppermute(computed, "feat", [(i, (i + o) % feat_groups) for i in range(feat_groups)])
            both = lax.dynamic_update_slice_in_dim(both, turned, ((x - o) % feat_groups) * part, 1)
        first = lax.dynamic_slice_in_dim(both[:, :HALO], x * cols, cols, 0).T
        return both, lax.ppermute(first, "atoms", [(i, (i - 1) % groups) for i in range(groups)])

    every, incoming = lax.cond(most <= room, one_pass, more_passes)
    every = every.T
    own = lax.dynamic_slice_in_dim(every, x * cols, cols, 1)
    future = jnp.concatenate([own[LAG:], incoming[:LAG]], 0)

    ids = jnp.concatenate([traj_ids[0], jnp.full((LAG,), -1, jnp.int32)])
    ids_now = lax.dynamic_slice_in_dim(ids, z * frames_here, frames_here)
    ids_later = lax.dynamic_slice_in_dim(ids, z * frames_here + LAG, frames_here)
    valid = (ids_now == ids_later).astype(jnp.float32)[:, None]

    count_b = jnp.sum(valid)
    inverse = 1.0 / jnp.maximum(count_b, 1.0)
    now_b = jnp.sum(valid * every, 0) * inverse
    next_b = jnp.sum(valid * future, 0) * inverse
    now_c = valid * (every - now_b)
    next_c = valid * (future - next_b)
    own_c = lax.dynamic_slice_in_dim(now_c, x * cols, cols, 1)
    stats = jnp.concatenate(
        [now_b, next_b, jnp.sum(now_c * now_c, 0), jnp.sum(next_c * next_c, 0), jnp.full((128,), count_b)]
    )
    reps = lax.axis_size("rep")
    stats = jnp.pad(stats, (0, -stats.shape[0] % 1024)).reshape(-1, 128)
    local = matmul(now_c, jnp.concatenate([own_c, next_c], 1), ((0,), (0,)), lax.Precision.HIGH)
    mine, stats = reduce_blocks(local, stats, groups, reps)
    stats = stats.reshape(groups * reps, -1)

    counts = stats[:, 2 * feats + 2 * cols :][:, :1]
    now_all = stats[:, :feats]
    next_all = stats[:, feats : feats + cols]
    sq_now = stats[:, feats + cols : 2 * feats + cols]
    sq_next = stats[:, 2 * feats + cols : 2 * feats + 2 * cols]
    count = jnp.sum(counts)
    mean_now = jnp.sum(counts * now_all, 0) / count
    mean_next = jnp.sum(counts * next_all, 0) / count
    off_now = now_all - mean_now
    off_next = next_all - mean_next
    spread_now = jnp.sum(sq_now + counts * off_now * off_now, 0)
    spread_next = jnp.sum(sq_next + counts * off_next * off_next, 0)
    scale_now = 1.0 / jnp.sqrt(spread_now / count + 1e-05)
    scale_next = 1.0 / jnp.sqrt(spread_next / count + 1e-05)

    rows = feats // lax.axis_size(("atoms", "rep"))
    row = lax.axis_index(("atoms", "rep")) * rows
    off_rows = lax.dynamic_slice_in_dim(off_now, row, rows, 1)
    off_cols = lax.dynamic_slice_in_dim(off_now, x * cols, cols, 1)
    mine = mine + matmul(
        counts * off_rows, jnp.concatenate([off_cols, off_next], 1), ((0,), (0,)), lax.Precision.HIGHEST
    )
    scale_rows = lax.dynamic_slice_in_dim(scale_now, row, rows)
    scale_cols = lax.dynamic_slice_in_dim(scale_now, x * cols, cols)
    mean_cols = lax.dynamic_slice_in_dim(mean_now, x * cols, cols)
    corr_inst = mine[:, :cols] / count * scale_rows[:, None] * scale_cols[None, :]
    corr_lag = mine[:, cols:] / count * scale_rows[:, None] * scale_next[None, :]
    projections = ((own - mean_cols) * scale_cols)[None]
    return (corr_inst, corr_lag, projections)


def solution(mesh):
    placed = (P(("grp", "rep"), None, None, "atoms"), P(None, "feat"), P(("grp", "rep"), None))
    return jax.shard_map(
        shards,
        mesh=mesh,
        in_specs=placed,
        out_specs=(
            P(("grp", "atoms", "rep"), "feat"),
            P(("grp", "atoms", "rep"), "feat"),
            P(("grp", "rep"), "atoms", "feat"),
        ),
        check_vma=False,
    )
```
